32 devices in a mesh: kc: 8 (over z, core), ia: 4 (over y, x).
Axes of the slice: x: 2, y: 2, z: 4, core: 2. Of those that a mesh axis runs over, the one named last changes fastest.
Arguments:
- amplitudes: bfloat16 [32768, 32768], P('ia', 'kc'), may hold values from -0.03125 to 0.03125
- occupied_factors: bfloat16 [2048, 4096], P('kc'), may hold values from -0.1875 to 0.1875
- virtual_factors: bfloat16 [2048, 4096], P('kc', 'ia'), may hold values from -6 to 6
Outputs:
- residual: float32 [32768, 512], P('ia', 'kc')
The draws below stay inside these ranges and needn't reach their ends.
All inputs are finite; a program needn't handle non-finite values.
Results may differ from the reference program's by a relative error of at most 0.0029.
Values may be sent and summed in bfloat16 or wider, within the bound.
A program may use at most 128 MiB of HBM per device.

```python
import jax
import jax.numpy as jnp
from jax import lax

O = 64
V = 512
Q = 2048
BW = 8


def spiked(array, stream_key, source, target, shards_of, factor):
    owner, partner = [(jnp.arange(array.shape[position]) // (array.shape[position] // shards_of)).reshape([-1 if axis == position else 1 for axis in range(array.ndim)]) for position in (source, target)]
    chosen = jax.random.permutation(stream_key, shards_of)[partner]
    strong = (owner == chosen) | (owner == (partner + shards_of // 2) % shards_of)
    return jnp.where(strong, factor * array, array)


def shard_levels(rng, dims, cuts, least, high):
    def one(axis_at, shards_of):
        steps = jax.random.uniform(jax.random.fold_in(jax.random.fold_in(rng, 6), axis_at), (shards_of,), jnp.float32, least / len(cuts), high / len(cuts))
        return jnp.repeat(jnp.exp(steps), dims[axis_at] // shards_of).reshape((-1,) + (1,) * (len(dims) - axis_at - 1))

    gain = one(*cuts[0])
    for cut in cuts[1:]:
        gain = gain * one(*cut)
    return gain


def gaussian(own_key, dims, deviation, most, split=(), held_as=jnp.bfloat16):
    values = jax.random.normal(own_key, dims, jnp.float32) * deviation
    if len(split) > 0:
        values = shard_levels(own_key, dims, split, -0.22, 0.18) * values
    return jnp.clip(values, min=-most, max=most).astype(held_as)


def heavy_noise(own_key, extent, width, bound, pieces, heavy, held_as=jnp.bfloat16):
    entries = width * jax.random.normal(own_key, extent, jnp.float32)
    if pieces:
        entries = entries * shard_levels(own_key, extent, pieces, -0.22, 0.18)
    return jnp.clip(spiked(entries, jax.random.fold_in(own_key, 3), *heavy), -bound, bound).astype(held_as)


def setup_inputs(seed: int = 0) -> dict:
    splits = jax.random.split(jax.random.key(seed), 4)
    return {
        "amplitudes": gaussian(splits[0], (O * V, O * V), (O * V) ** -0.5, 0.03125, ((0, 4), (1, 8))),
        "occupied_factors": heavy_noise(splits[1], (Q, O * O), Q ** -0.5, 0.1875, ((0, 8),), (0, 1, 8, 2.0)),
        "virtual_factors": gaussian(splits[2], (Q, V * BW), 1.0, 6.0, ((0, 8), (1, 4))),
    }


def reference(amplitudes, occupied_factors, virtual_factors):
    integrals = jnp.dot(occupied_factors.T, virtual_factors, preferred_element_type=jnp.float32).astype(jnp.bfloat16)
    cycle_block = integrals.reshape(O, O, V, BW).transpose(0, 2, 1, 3).reshape(O * V, O * BW)

    def one_block(amplitude_rows):
        return jnp.dot(amplitude_rows, cycle_block, preferred_element_type=jnp.float32)

    blocks = lax.map(one_block, amplitudes.reshape(O, V, O * V))
    return blocks.reshape(O * V, O * BW)
```

```python
import functools

import jax
import jax.numpy as jnp
import numpy as np
from jax import lax
from jax.experimental import pallas as pl
from jax.experimental.pallas import tpu as pltpu
from jax.sharding import PartitionSpec as P

O = 64
V = 512
BW = 8
QUARTERS = 4
LANES = 128
MESH = pl.DeviceIdType.MESH
BF, F32 = jnp.bfloat16, jnp.float32


class Spread:
    def __init__(self, view, kind, groups, send, recv):
        self.view, self.kind, self.send, self.recv = view, kind, send, recv
        self.a = 2
        self.b = groups // 2
        me = lax.axis_index("ia")
        self.p, self.q = me // self.b, me % self.b

    def at(self, r, s):
        return lax.rem(self.p + s + self.a, self.a) * self.b + lax.rem(self.q + r + self.b, self.b)

    def copy(self, source, r, s, target):
        place = self.view(self.at(*source))
        return pltpu.make_async_remote_copy(
            src_ref=place, dst_ref=place, send_sem=self.send.at[r, s],
            recv_sem=self.recv.at[r, s], device_id={"ia": self.at(*target)}, device_id_type=MESH)

    def sends(self, direct):
        out = []
        for r in range(self.b):
            for s in range(self.a):
                if r and s and not direct:
                    out.append(self.copy((-r, 0), r, s, (0, s)) if self.kind == 0
                               else self.copy((0, -s), r, s, (r, 0)))
                elif (r or s) and not (r and s) and direct:
                    out.append(self.copy((0, 0), r, s, (r, s)))
        return out

    def arrived(self, r, s):
        place = self.view(self.at(-r, -s))
        pltpu.make_async_remote_copy(
            src_ref=place, dst_ref=place, send_sem=self.send.at[r, s], recv_sem=self.recv.at[r, s],
            device_id={"ia": self.at(r, s)}, device_id_type=MESH).wait_recv()

    def start(self):
        order = self.sends(True)
        for copy in order if self.kind else reversed(order):
            copy.start()

    def relay(self):
        if self.kind == 0:
            for r in range(1, self.b):
                self.arrived(r, 0)
        else:
            for s in range(1, self.a):
                self.arrived(0, s)
        for copy in self.sends(False):
            copy.start()

    def finish(self):
        for r in range(self.b):
            for s in range(self.a):
                first = (s == 0) if self.kind == 0 else (r == 0)
                if (r or s) and not first:
                    self.arrived(r, s)

    def drain(self):
        for copy in self.sends(True) + self.sends(False):
            copy.wait_send()


def signal_all(barrier, axis, size):
    me = lax.axis_index(axis)
    for step in range(1, size):
        pl.semaphore_signal(barrier, inc=1, device_id={axis: lax.rem(me + step, size)}, device_id_type=MESH)


def choices(c_dim, j_own):
    per_q, together = BW // QUARTERS, LANES // O
    b, c = np.divmod(np.arange(BW * c_dim), c_dim)
    by_b = np.zeros((BW * c_dim, BW * c_dim), np.float32)
    by_b[np.arange(BW * c_dim), c * BW + b] = 1
    at = np.arange(per_q * LANES)
    b, k, j = at // LANES, at // O % together, at % O
    place = np.zeros((per_q * LANES, together * LANES), np.float32)
    place[at, k * LANES + j // j_own * (per_q * j_own) + b * j_own + j % j_own] = 1
    return jnp.asarray(by_b, BF), jnp.asarray(place, BF)


def cycle_kernel(
    devices, groups, count, rows, first, depth, lag,
    a_ref, occ_ref, virt_ref, by_b_ref, place_ref, o_ref,
    by_b, place, piece, vbuf, vt, occ, cyc, abuf, pair_out, pair_in, total, out, arr, kept, given,
    load_sem, mine_s, o_s, o_r, g_s, g_r, right_s, left_s, v_r, vp_s, vp_r, c_s, c_r,
    a_sem, p_s, p_r, rr_s, rr_r, ll_s, ll_r, kept_sem, given_s, given_r,
):
    n = devices // 2
    me, ia = lax.axis_index("kc"), lax.axis_index("ia")
    z, core = me // 2, me % 2
    other = 1 - core
    partner = z * 2 + other
    q_dim, columns = virt_ref.shape
    per_q = BW // QUARTERS
    c_dim = columns // BW
    q_rows = per_q * c_dim
    share = occ_ref.shape[0] // groups
    cols = occ_ref.shape[1] // devices
    k_dim = cyc.shape[0]
    j_own = O // devices
    w = 2 * per_q * j_own
    half = w // 2
    steps = 2 * count
    ring = total.shape[0]

    def fetch(f):
        slot = lax.rem(f, depth)
        t = lax.rem(f // 2, count)
        chunk = 2 * t + jnp.where(lax.rem(f, 2) == 0, other, core)
        start = pl.multiple_of(chunk * rows, rows)
        return pltpu.make_async_copy(a_ref.at[pl.ds(start, rows)], abuf.at[slot], a_sem.at[slot])

    def lanes_of(device):
        return pl.ds(pl.multiple_of(device * q_dim, q_dim), q_dim)

    def rows_of(q):
        return pl.ds(pl.multiple_of(q * q_rows, q_rows), q_rows)

    def virtual(q, chip, way):
        place = vt.at[rows_of(q), lanes_of(chip * 2 + core)]
        send = {"right": right_s, "left": left_s, "pair": vp_s}[way]
        to = {"right": me + 2, "left": me - 2, "pair": partner}[way]
        recv = vp_r if way == "pair" else v_r
        return pltpu.make_async_remote_copy(
            src_ref=place, dst_ref=place, send_sem=send.at[q, chip],
            recv_sem=recv.at[q, chip], device_id={"kc": to}, device_id_type=MESH)

    def pair_came(q, chip):
        place = vt.at[rows_of(q), lanes_of(chip * 2 + other)]
        pltpu.make_async_remote_copy(
            src_ref=place, dst_ref=place, send_sem=vp_s.at[q, chip], recv_sem=vp_r.at[q, chip],
            device_id={"kc": partner}, device_id_type=MESH).wait_recv()

    def prepare(q, carry):
        vt[rows_of(q), lanes_of(me)] = lax.dot_general(
            by_b[rows_of(q)], vbuf[...], (((1,), (1,)), ((), ())), preferred_element_type=F32).astype(BF)
        return carry

    def send_own(q):
        @pl.when(z < n - 1)
        def _():
            virtual(q, z, "right").start()

        @pl.when(z > 0)
        def _():
            virtual(q, z, "left").start()

        virtual(q, z, "pair").start()

    def hop(q, step):
        @pl.when(z - step >= 0)
        def _():
            virtual(q, z - step, "left").wait_recv()

            @pl.when(z < n - 1)
            def _():
                virtual(q, z - step, "right").start()

            virtual(q, z - step, "pair").start()

        @pl.when(z + step < n)
        def _():
            virtual(q, z + step, "left").wait_recv()

            @pl.when(z > 0)
            def _():
                virtual(q, z + step, "left").start()

            virtual(q, z + step, "pair").start()

    def hops(begin, end):
        def body(h, carry):
            q, dist = h // (n - 1), lax.rem(h, n - 1) + 1
            hop(q, dist)

            @pl.when((dist == 1) & (q < QUARTERS - 1))
            def _():
                send_own(q + 1)

            return carry

        lax.fori_loop(begin, end, body, 0)

    def share_of(i):
        return pl.ds(pl.multiple_of(i * share, share), share)

    def direct(to):
        return pltpu.make_async_remote_copy(
            src_ref=occ_ref.at[pl.ds(pl.multiple_of(ia * share, share), share),
                               pl.ds(pl.multiple_of(to * cols, cols), cols)],
            dst_ref=occ.at[me, share_of(ia)], send_sem=o_s.at[to], recv_sem=o_r.at[me],
            device_id={"kc": to}, device_id_type=MESH)

    def came(source):
        place = occ.at[source, share_of(ia)]
        pltpu.make_async_remote_copy(
            src_ref=place, dst_ref=place, send_sem=o_s.at[source],
            recv_sem=o_r.at[source], device_id={"kc": source}, device_id_type=MESH).wait_recv()

    def to_partner():
        return pltpu.make_async_remote_copy(
            src_ref=occ_ref.at[:, pl.ds(pl.multiple_of(partner * cols, cols), cols)],
            dst_ref=occ.at[me], send_sem=o_s.at[partner], recv_sem=o_r.at[me],
            device_id={"kc": partner}, device_id_type=MESH)

    def partner_came():
        pltpu.make_async_remote_copy(
            src_ref=occ.at[partner], dst_ref=occ.at[partner], send_sem=o_s.at[partner],
            recv_sem=o_r.at[partner], device_id={"kc": partner}, device_id_type=MESH).wait_recv()

    def side(e, act):
        chip = z + (2 * lax.rem(e, 2) - 1) * (lax.div(e, 2) + 1)

        @pl.when((e >= 0) & (chip >= 0) & (chip < n))
        def _():
            act(chip * 2 + core, 0)
            act(chip * 2 + other, 1)

    def sides(*acts):
        def body(e, carry):
            for act in acts:
                side(e, act)
            return carry

        lax.fori_loop(0, 2 * (n - 1), body, 0)

    def occ_spread(source, kind):
        view = functools.partial(lambda source, i: occ.at[source, share_of(i)], source)
        return Spread(view, kind, groups, g_s.at[source], g_r.at[source])

    def occ_start(source, kind):
        came(source)
        occ_spread(source, kind).start()

    def lanes(q, size=1):
        start = q * LANES
        return pl.ds(start if isinstance(q, int) else pl.multiple_of(start, LANES), size * LANES)

    def cycle_spreads(q):
        out = []
        for kind in range(2):
            ks = pl.ds(kind * (k_dim // 2), k_dim // 2)
            view = functools.partial(
                lambda ks, i: cyc.at[ks, i, :, lanes(q)], ks)
            out.append(Spread(view, kind, groups, c_s.at[q, kind], c_r.at[q, kind]))
        return out

    def each(q, what):
        for spread in cycle_spreads(q):
            getattr(spread, what)()

    def integrals(q):
        def waits(chip, carry):
            pair_came(q, chip)
            return carry

        lax.fori_loop(0, n, waits, 0)
        block = jnp.dot(
            vt[rows_of(q), :], occ[...].reshape(-1, cols), preferred_element_type=F32).astype(BF)
        together = LANES // O
        for k in range(0, k_dim, together):
            for b in range(per_q):
                piece[:, b * LANES:(b + 1) * LANES] = block[b * c_dim:(b + 1) * c_dim, k * O:(k + together) * O]
            laid = jnp.dot(piece[...], place[...], preferred_element_type=F32).astype(BF)
            for i in range(together):
                cyc[k + i, ia, :, lanes(q)] = laid[:, i * LANES:(i + 1) * LANES]

    def pair(g, t, qs):
        return pltpu.make_async_remote_copy(
            src_ref=pair_out.at[t, qs], dst_ref=pair_in.at[t, qs], send_sem=p_s.at[g],
            recv_sem=p_r.at[g], device_id={"kc": partner}, device_id_type=MESH)

    def multiply(g, t, qs):
        slot = lax.rem(g, ring)

        def one(i, carry):
            f = 2 * g + i
            fetch(f).wait()

            @pl.when(f + depth - 1 < 2 * steps)
            def _():
                fetch(f + depth - 1).start()

            made = jnp.dot(
                abuf[lax.rem(f, depth)],
                cyc[:, :, :, lanes(qs.start, qs.size)].reshape(-1, qs.size * LANES),
                preferred_element_type=F32)

            @pl.when(i == 0)
            def _():
                for q in range(qs.size):
                    pair_out[t, qs.start + q] = made[:, q * LANES:(q + 1) * LANES].astype(BF)
                pair(g, t, qs).start()

            @pl.when(i == 1)
            def _():
                pair(g, t, qs).wait_recv()
                for q in range(qs.size):
                    both = made[:, q * LANES:(q + 1) * LANES] + pair_in[t, qs.start + q].astype(F32)
                    total[slot, q] = both.T

            return carry

        lax.fori_loop(0, 2, one, 0)

    def go_right(g, t, qs, zz):
        return pltpu.make_async_remote_copy(
            src_ref=out.at[t, qs, pl.ds((zz + 1) * w, (n - 1 - zz) * w)],
            dst_ref=arr.at[t, qs, pl.ds((zz + 2) * w, (n - 1 - zz) * w)],
            send_sem=rr_s.at[g], recv_sem=rr_r.at[g], device_id={"kc": me + 2}, device_id_type=MESH)

    def go_left(g, t, qs, zz):
        return pltpu.make_async_remote_copy(
            src_ref=out.at[t, qs, pl.ds(0, zz * w)], dst_ref=arr.at[t, qs, pl.ds(0, zz * w)],
            send_sem=ll_s.at[g], recv_sem=ll_r.at[g], device_id={"kc": me - 2}, device_id_type=MESH)

    def from_left(g, t, qs, zz):
        place = arr.at[t, qs, pl.ds((zz + 1) * w, (n - zz) * w)]
        pltpu.make_async_remote_copy(
            src_ref=place, dst_ref=place, send_sem=rr_s.at[g], recv_sem=rr_r.at[g],
            device_id={"kc": me - 2}, device_id_type=MESH).wait_recv()

    def from_right(g, t, qs, zz):
        place = arr.at[t, qs, pl.ds(0, (zz + 1) * w)]
        pltpu.make_async_remote_copy(
            src_ref=place, dst_ref=place, send_sem=ll_s.at[g], recv_sem=ll_r.at[g],
            device_id={"kc": me + 2}, device_id_type=MESH).wait_recv()

    def in_segment(g, act):
        t = lax.rem(g, count)
        for size, here, low in (
            (1, (g >= 0) & (g < first), 0),
            (2, ((g >= first) & (g < count)) | ((g >= count + first) & (g < steps)),
             jnp.where(g >= count, 2, 0)),
            (3, (g >= count) & (g < count + first), 1),
        ):
            @pl.when(here)
            def _():
                act(t, pl.ds(low, size))

    def at_place(g, act):
        def body(t, qs):
            mine = total.at[lax.rem(g, ring), pl.ds(0, qs.size)]
            for zz in range(n):
                @pl.when(z == zz)
                def _():
                    act(g, t, qs, mine, zz)

        in_segment(g, body)

    def rightwards(g, t, qs, mine, zz):
        if zz == n - 1:
            return
        value = mine[:, (zz + 1) * w:, :]
        if zz > 0:
            from_left(g, t, qs, zz)
            value += arr[t, qs, (zz + 2) * w:, :].astype(F32)
        out[t, qs, (zz + 1) * w:, :] = value.astype(BF)
        go_right(g, t, qs, zz).start()

    def leftwards(g, t, qs, mine, zz):
        if zz == 0:
            return
        value = mine[:, :zz * w, :]
        if zz < n - 1:
            from_right(g, t, qs, zz)
            value += arr[t, qs, :zz * w, :].astype(F32)
        out[t, qs, :zz * w, :] = value.astype(BF)
        go_left(g, t, qs, zz).start()

    def columns_of(t, whose):
        return pl.ds(pl.multiple_of((2 * t + whose) * rows, rows), rows)

    def keep(g, t, qs):
        return pltpu.make_async_copy(
            kept.at[t, qs], o_ref.at[qs, :, columns_of(t, core)], kept_sem.at[g])

    def give(g, t, qs, whose):
        return pltpu.make_async_remote_copy(
            src_ref=given.at[t, qs], dst_ref=o_ref.at[qs, :, columns_of(t, whose)],
            send_sem=given_s.at[g], recv_sem=given_r.at[g],
            device_id={"kc": partner}, device_id_type=MESH)

    def final(g, t, qs, mine, zz):
        value = mine[:, zz * w:(zz + 1) * w, :]
        if zz == n - 1:
            from_left(g, t, qs, zz)
        if zz > 0:
            value += arr[t, qs, (zz + 1) * w:(zz + 2) * w, :].astype(F32)
        if zz == 0:
            from_right(g, t, qs, zz)
        if zz < n - 1:
            value += arr[t, qs, zz * w:(zz + 1) * w, :].astype(F32)

        @pl.when(core == 0)
        def _():
            kept[t, qs] = value[:, :half]
            given[t, qs] = value[:, half:]

        @pl.when(core == 1)
        def _():
            kept[t, qs] = value[:, half:]
            given[t, qs] = value[:, :half]

    def hand_over(g):
        def body(t, qs):
            keep(g, t, qs).start()
            give(g, t, qs, core).start()

        in_segment(g, body)

    loads = [
        pltpu.make_async_copy(source, target, load_sem.at[i])
        for i, (source, target) in enumerate(((virt_ref, vbuf), (by_b_ref, by_b), (place_ref, place)))
    ]
    for load in loads:
        load.start()
    barrier = pltpu.get_barrier_semaphore()
    signal_all(barrier, "kc", devices)
    signal_all(barrier, "ia", groups)
    mine = pltpu.make_async_copy(
        occ_ref.at[:, pl.ds(pl.multiple_of(me * cols, cols), cols)], occ.at[me], mine_s)
    for load in loads:
        load.wait()
    lax.fori_loop(0, QUARTERS, prepare, 0)
    pl.semaphore_wait(barrier, devices + groups - 2)

    sides(lambda to, kind: direct(to).start())
    send_own(0)
    to_partner().start()
    mine.start()
    for f in range(depth - 1):
        fetch(f).start()

    def occ_step(e, carry):
        side(e, occ_start)
        side(e - 2, lambda source, kind: occ_spread(source, kind).relay())
        return carry

    lax.fori_loop(0, 2 * n, occ_step, 0)
    hops(0, n)
    partner_came()
    sides(lambda source, kind: occ_spread(source, kind).finish())
    mine.wait()

    hop_plan = [(1, 2 * n - 1), (2, 3 * n - 4), (3, 3 * n - 2), (first + 1, 3 * n - 1), (first + 4, 4 * n - 4)]
    relays = [1, 3, first + 3, first + 6]
    makes = [0, 1, 3, first + 4]
    finishes = [1, first + 2, first + 6, count + 2]

    def hops_until(i, after):
        done = most = n
        for at, upto in hop_plan:
            most = max(most, min(upto, QUARTERS * (n - 1)))
            done = jnp.where((i > at) if after else (i >= at), most, done)
        return done

    def at_events(i, events, act):
        here, q = i == events[0], 0
        for later, at in enumerate(events[1:], 1):
            here = here | (i == at)
            q = q + jnp.where(i == at, later, 0)

        @pl.when(here)
        def _():
            act(q)

    def make(q):
        integrals(q)
        each(q, "start")

    def step(i, carry):
        g = i - 2
        at_events(i, relays, lambda q: each(q, "relay"))
        hops(hops_until(i, True), hops_until(i, False))
        at_events(i, makes, make)
        at_events(i, finishes, lambda q: each(q, "finish"))
        in_segment(g, lambda t, qs: multiply(g, t, qs))
        at_place(g - z, rightwards)
        at_place(g - (n - 1 - z), leftwards)
        at_place(g - lag, final)
        hand_over(g - lag)
        return carry

    lax.fori_loop(0, steps + lag + 2, step, 0)

    def drain(g, carry):
        def body(t, qs):
            pair(g, t, qs).wait_send()
            keep(g, t, qs).wait()
            give(g, t, qs, core).wait_send()
            give(g, t, qs, other).wait_recv()
            for zz in range(n):
                @pl.when(z == zz)
                def _():
                    if zz < n - 1:
                        go_right(g, t, qs, zz).wait_send()
                    if zz > 0:
                        go_left(g, t, qs, zz).wait_send()

        in_segment(g, body)
        return carry

    lax.fori_loop(0, steps, drain, 0)
    to_partner().wait_send()
    sides(
        lambda to, kind: direct(to).wait_send(),
        lambda source, kind: occ_spread(source, kind).drain())

    def drain_factors(i, carry):
        q, chip = lax.div(i, n), lax.rem(i, n)
        virtual(q, chip, "pair").wait_send()

        @pl.when((chip <= z) & (z < n - 1))
        def _():
            virtual(q, chip, "right").wait_send()

        @pl.when((chip >= z) & (z > 0))
        def _():
            virtual(q, chip, "left").wait_send()

        @pl.when(chip == 0)
        def _():
            each(q, "drain")

        return carry

    lax.fori_loop(0, QUARTERS * n, drain_factors, 0)


def per_device(amplitudes, occupied, virtual):
    devices, groups = lax.axis_size("kc"), lax.axis_size("ia")
    n = devices // 2
    local_rows, k_width = amplitudes.shape
    q_dim, columns = virtual.shape
    cols = occupied.shape[1] // devices
    k_dim, c_dim, j_own = O // devices, columns // BW, O // devices
    rows = min(512, local_rows // 16)
    count = local_rows // (2 * rows)
    first = (3 * count) // 8
    depth = 4
    lag = n
    width = n * 2 * (BW // QUARTERS) * j_own
    w = width // n
    dma = pltpu.SemaphoreType.DMA
    hbm = pl.BlockSpec(memory_space=pl.ANY)
    unit = (count, QUARTERS)
    by_b, place = choices(c_dim, j_own)
    result = pl.pallas_call(
        functools.partial(cycle_kernel, devices, groups, count, rows, first, depth, lag),
        out_shape=jax.ShapeDtypeStruct((QUARTERS, w // 2, local_rows), F32),
        in_specs=[hbm] * 5,
        out_specs=hbm,
        scratch_shapes=[
            pltpu.VMEM(by_b.shape, BF),
            pltpu.VMEM(place.shape, BF),
            pltpu.VMEM((c_dim, place.shape[0]), BF),
            pltpu.VMEM((q_dim, columns), BF),
            pltpu.VMEM((columns, devices * q_dim), BF),
            pltpu.VMEM((devices, q_dim, cols), BF),
            pltpu.VMEM((k_dim, groups, c_dim, O * BW), BF),
            pltpu.VMEM((depth, rows, k_width), BF),
            pltpu.VMEM(unit + (rows, LANES), BF),
            pltpu.VMEM(unit + (rows, LANES), BF),
            pltpu.VMEM((lag + 1, 3, width, rows), F32),
            pltpu.VMEM(unit + (width, rows), BF),
            pltpu.VMEM(unit + (width + w, rows), BF),
            pltpu.VMEM(unit + (w // 2, rows), F32),
            pltpu.VMEM(unit + (w // 2, rows), F32),
            dma((3,)), dma(()), dma((devices,)), dma((devices,)),
            dma((devices, groups // 2, 2)), dma((devices, groups // 2, 2)),
            dma((QUARTERS, n)), dma((QUARTERS, n)), dma((QUARTERS, n)), dma((QUARTERS, n)), dma((QUARTERS, n)),
            dma((QUARTERS, 2, groups // 2, 2)), dma((QUARTERS, 2, groups // 2, 2)),
            dma((depth,)),
        ] + [dma((2 * count,))] * 9,
        compiler_params=pltpu.CompilerParams(
            collective_id=0, has_side_effects=True, vmem_limit_bytes=60 * 2**20),
    )(amplitudes, occupied, virtual, by_b, place)
    return result.reshape(BW, j_own, local_rows).transpose(2, 1, 0).reshape(local_rows, j_own * BW)


def solution(mesh):
    placed = (P("ia", "kc"), P("kc", None), P("kc", "ia"))
    return jax.shard_map(
        per_device, mesh=mesh, in_specs=placed, out_specs=P("ia", "kc"), check_vma=False
    )
```

```python
import functools

import jax
import jax.numpy as jnp
import numpy as np
from jax import lax
from jax.experimental import pallas as pl
from jax.experimental.pallas import tpu as pltpu
from jax.sharding import PartitionSpec as P

O = 64
V = 512
BW = 8
QUARTERS = 4
LANES = 128
MESH = pl.DeviceIdType.MESH
BF, F32 = jnp.bfloat16, jnp.float32


class Spread:
    def __init__(self, view, kind, groups, send, recv):
        self.view, self.kind, self.send, self.recv = view, kind, send, recv
        self.a = 2
        self.b = groups // 2
        me = lax.axis_index("ia")
        self.p, self.q = me // self.b, me % self.b

    def at(self, r, s):
        return lax.rem(self.p + s + self.a, self.a) * self.b + lax.rem(self.q + r + self.b, self.b)

    def copy(self, source, r, s, target):
        place = self.view(self.at(*source))
        return pltpu.make_async_remote_copy(
            src_ref=place, dst_ref=place, send_sem=self.send.at[r, s],
            recv_sem=self.recv.at[r, s], device_id={"ia": self.at(*target)}, device_id_type=MESH)

    def sends(self, direct):
        out = []
        for r in range(self.b):
            for s in range(self.a):
                if r and s and not direct:
                    out.append(self.copy((-r, 0), r, s, (0, s)) if self.kind == 0
                               else self.copy((0, -s), r, s, (r, 0)))
                elif (r or s) and not (r and s) and direct:
                    out.append(self.copy((0, 0), r, s, (r, s)))
        return out

    def arrived(self, r, s):
        place = self.view(self.at(-r, -s))
        pltpu.make_async_remote_copy(
            src_ref=place, dst_ref=place, send_sem=self.send.at[r, s], recv_sem=self.recv.at[r, s],
            device_id={"ia": self.at(r, s)}, device_id_type=MESH).wait_recv()

    def start(self):
        order = self.sends(True)
        for copy in order if self.kind else reversed(order):
            copy.start()

    def relay(self):
        if self.kind == 0:
            for r in range(1, self.b):
                self.arrived(r, 0)
        else:
            for s in range(1, self.a):
                self.arrived(0, s)
        for copy in self.sends(False):
            copy.start()

    def finish(self):
        for r in range(self.b):
            for s in range(self.a):
                first = (s == 0) if self.kind == 0 else (r == 0)
                if (r or s) and not first:
                    self.arrived(r, s)

    def drain(self):
        for copy in self.sends(True) + self.sends(False):
            copy.wait_send()


class Direct(Spread):
    def sends(self, direct):
        return [self.copy((0, 0), r, s, (r, s)) for r in range(self.b) for s in range(self.a) if r or s] if direct else []

    def start(self):
        for copy in self.sends(True):
            copy.start()

    def relay(self):
        pass

    def finish(self):
        for r in range(self.b):
            for s in range(self.a):
                if r or s:
                    self.arrived(r, s)


def signal_all(barrier, axis, size):
    me = lax.axis_index(axis)
    for step in range(1, size):
        pl.semaphore_signal(barrier, inc=1, device_id={axis: lax.rem(me + step, size)}, device_id_type=MESH)


def choices(c_dim, j_own):
    per_q, together = BW // QUARTERS, LANES // O
    b, c = np.divmod(np.arange(BW * c_dim), c_dim)
    by_b = np.zeros((BW * c_dim, BW * c_dim), np.float32)
    by_b[np.arange(BW * c_dim), c * BW + b] = 1
    at = np.arange(per_q * LANES)
    b, k, j = at // LANES, at // O % together, at % O
    place = np.zeros((per_q * LANES, together * LANES), np.float32)
    place[at, k * LANES + j // j_own * (per_q * j_own) + b * j_own + j % j_own] = 1
    return jnp.asarray(by_b, BF), jnp.asarray(place, BF)


def cycle_kernel(
    devices, groups, count, rows, first, depth, lag,
    a_ref, occ_ref, virt_ref, by_b_ref, place_ref, o_ref,
    by_b, place, piece, vbuf, vt, occ, cyc, abuf, pair_out, pair_in, total, out, arr, kept, given,
    load_sem, mine_s, o_s, o_r, g_s, g_r, right_s, left_s, v_r, vp_s, vp_r, c_s, c_r,
    a_sem, p_s, p_r, rr_s, rr_r, ll_s, ll_r, kept_sem, given_s, given_r,
):
    n = devices // 2
    me, ia = lax.axis_index("kc"), lax.axis_index("ia")
    z, core = me // 2, me % 2
    other = 1 - core
    partner = z * 2 + other
    q_dim, columns = virt_ref.shape
    per_q = BW // QUARTERS
    c_dim = columns // BW
    q_rows = per_q * c_dim
    share = occ_ref.shape[0] // groups
    cols = occ_ref.shape[1] // devices
    k_dim = cyc.shape[0]
    j_own = O // devices
    w = 2 * per_q * j_own
    half = w // 2
    steps = 2 * count
    ring = total.shape[0]

    def fetch(f):
        slot = lax.rem(f, depth)
        t = lax.rem(f // 2, count)
        chunk = 2 * t + jnp.where(lax.rem(f, 2) == 0, other, core)
        start = pl.multiple_of(chunk * rows, rows)
        return pltpu.make_async_copy(a_ref.at[pl.ds(start, rows)], abuf.at[slot], a_sem.at[slot])

    def lanes_of(device):
        return pl.ds(pl.multiple_of(device * q_dim, q_dim), q_dim)

    def rows_of(q):
        return pl.ds(pl.multiple_of(q * q_rows, q_rows), q_rows)

    def virtual(q, chip, way):
        place = vt.at[rows_of(q), lanes_of(chip * 2 + core)]
        send = {"right": right_s, "left": left_s, "pair": vp_s}[way]
        to = {"right": me + 2, "left": me - 2, "pair": partner}[way]
        recv = vp_r if way == "pair" else v_r
        return pltpu.make_async_remote_copy(
            src_ref=place, dst_ref=place, send_sem=send.at[q, chip],
            recv_sem=recv.at[q, chip], device_id={"kc": to}, device_id_type=MESH)

    def pair_came(q, chip):
        place = vt.at[rows_of(q), lanes_of(chip * 2 + other)]
        pltpu.make_async_remote_copy(
            src_ref=place, dst_ref=place, send_sem=vp_s.at[q, chip], recv_sem=vp_r.at[q, chip],
            device_id={"kc": partner}, device_id_type=MESH).wait_recv()

    def prepare(q, carry):
        vt[rows_of(q), lanes_of(me)] = lax.dot_general(
            by_b[rows_of(q)], vbuf[...], (((1,), (1,)), ((), ())), preferred_element_type=F32).astype(BF)
        return carry

    def send_own(q):
        @pl.when(z < n - 1)
        def _():
            virtual(q, z, "right").start()

        @pl.when(z > 0)
        def _():
            virtual(q, z, "left").start()

        virtual(q, z, "pair").start()

    def hop(q, step):
        @pl.when(z - step >= 0)
        def _():
            virtual(q, z - step, "left").wait_recv()

            @pl.when(z < n - 1)
            def _():
                virtual(q, z - step, "right").start()

            virtual(q, z - step, "pair").start()

        @pl.when(z + step < n)
        def _():
            virtual(q, z + step, "left").wait_recv()

            @pl.when(z > 0)
            def _():
                virtual(q, z + step, "left").start()

            virtual(q, z + step, "pair").start()

    def hops(begin, end):
        def body(h, carry):
            q, dist = h // (n - 1), lax.rem(h, n - 1) + 1
            hop(q, dist)

            @pl.when((dist == 1) & (q < QUARTERS - 1))
            def _():
                send_own(q + 1)

            return carry

        lax.fori_loop(begin, end, body, 0)

    def share_of(i):
        return pl.ds(pl.multiple_of(i * share, share), share)

    def direct(to):
        return pltpu.make_async_remote_copy(
            src_ref=occ_ref.at[pl.ds(pl.multiple_of(ia * share, share), share),
                               pl.ds(pl.multiple_of(to * cols, cols), cols)],
            dst_ref=occ.at[me, share_of(ia)], send_sem=o_s.at[to], recv_sem=o_r.at[me],
            device_id={"kc": to}, device_id_type=MESH)

    def came(source):
        place = occ.at[source, share_of(ia)]
        pltpu.make_async_remote_copy(
            src_ref=place, dst_ref=place, send_sem=o_s.at[source],
            recv_sem=o_r.at[source], device_id={"kc": source}, device_id_type=MESH).wait_recv()

    def to_partner():
        return pltpu.make_async_remote_copy(
            src_ref=occ_ref.at[:, pl.ds(pl.multiple_of(partner * cols, cols), cols)],
            dst_ref=occ.at[me], send_sem=o_s.at[partner], recv_sem=o_r.at[me],
            device_id={"kc": partner}, device_id_type=MESH)

    def partner_came():
        pltpu.make_async_remote_copy(
            src_ref=occ.at[partner], dst_ref=occ.at[partner], send_sem=o_s.at[partner],
            recv_sem=o_r.at[partner], device_id={"kc": partner}, device_id_type=MESH).wait_recv()

    def side(e, act):
        chip = z + (2 * lax.rem(e, 2) - 1) * (lax.div(e, 2) + 1)

        @pl.when((e >= 0) & (chip >= 0) & (chip < n))
        def _():
            act(chip * 2 + core, 0)
            act(chip * 2 + other, 1)

    def sides(*acts):
        def body(e, carry):
            for act in acts:
                side(e, act)
            return carry

        lax.fori_loop(0, 2 * (n - 1), body, 0)

    def occ_spread(source, kind):
        view = functools.partial(lambda source, i: occ.at[source, share_of(i)], source)
        return Direct(view, kind, groups, g_s.at[source], g_r.at[source])

    def occ_start(source, kind):
        came(source)
        occ_spread(source, kind).start()

    def lanes(q, size=1):
        start = q * LANES
        return pl.ds(start if isinstance(q, int) else pl.multiple_of(start, LANES), size * LANES)

    def cycle_spreads(q):
        out = []
        for kind in range(2):
            ks = pl.ds(kind * (k_dim // 2), k_dim // 2)
            view = functools.partial(
                lambda ks, i: cyc.at[ks, i, :, lanes(q)], ks)
            out.append(Spread(view, kind, groups, c_s.at[q, kind], c_r.at[q, kind]))
        return out

    def each(q, what):
        for spread in cycle_spreads(q):
            getattr(spread, what)()

    def integrals(q):
        def waits(chip, carry):
            pair_came(q, chip)
            return carry

        lax.fori_loop(0, n, waits, 0)
        block = jnp.dot(
            vt[rows_of(q), :], occ[...].reshape(-1, cols), preferred_element_type=F32).astype(BF)
        together = LANES // O
        for k in range(0, k_dim, together):
            for b in range(per_q):
                piece[:, b * LANES:(b + 1) * LANES] = block[b * c_dim:(b + 1) * c_dim, k * O:(k + together) * O]
            laid = jnp.dot(piece[...], place[...], preferred_element_type=F32).astype(BF)
            for i in range(together):
                cyc[k + i, ia, :, lanes(q)] = laid[:, i * LANES:(i + 1) * LANES]

    def pair(g, t, qs):
        return pltpu.make_async_remote_copy(
            src_ref=pair_out.at[t, qs], dst_ref=pair_in.at[t, qs], send_sem=p_s.at[g],
            recv_sem=p_r.at[g], device_id={"kc": partner}, device_id_type=MESH)

    def multiply(g, t, qs):
        slot = lax.rem(g, ring)

        def one(i, carry):
            f = 2 * g + i
            fetch(f).wait()

            @pl.when(f + depth - 1 < 2 * steps)
            def _():
                fetch(f + depth - 1).start()

            made = jnp.dot(
                abuf[lax.rem(f, depth)],
                cyc[:, :, :, lanes(qs.start, qs.size)].reshape(-1, qs.size * LANES),
                preferred_element_type=F32)

            @pl.when(i == 0)
            def _():
                for q in range(qs.size):
                    pair_out[t, qs.start + q] = made[:, q * LANES:(q + 1) * LANES].astype(BF)
                pair(g, t, qs).start()

            @pl.when(i == 1)
            def _():
                pair(g, t, qs).wait_recv()
                for q in range(qs.size):
                    both = made[:, q * LANES:(q + 1) * LANES] + pair_in[t, qs.start + q].astype(F32)
                    total[slot, q] = both.T

            return carry

        lax.fori_loop(0, 2, one, 0)

    def go_right(g, t, qs, zz):
        return pltpu.make_async_remote_copy(
            src_ref=out.at[t, qs, pl.ds((zz + 1) * w, (n - 1 - zz) * w)],
            dst_ref=arr.at[t, qs, pl.ds((zz + 2) * w, (n - 1 - zz) * w)],
            send_sem=rr_s.at[g], recv_sem=rr_r.at[g], device_id={"kc": me + 2}, device_id_type=MESH)

    def go_left(g, t, qs, zz):
        return pltpu.make_async_remote_copy(
            src_ref=out.at[t, qs, pl.ds(0, zz * w)], dst_ref=arr.at[t, qs, pl.ds(0, zz * w)],
            send_sem=ll_s.at[g], recv_sem=ll_r.at[g], device_id={"kc": me - 2}, device_id_type=MESH)

    def from_left(g, t, qs, zz):
        place = arr.at[t, qs, pl.ds((zz + 1) * w, (n - zz) * w)]
        pltpu.make_async_remote_copy(
            src_ref=place, dst_ref=place, send_sem=rr_s.at[g], recv_sem=rr_r.at[g],
            device_id={"kc": me - 2}, device_id_type=MESH).wait_recv()

    def from_right(g, t, qs, zz):
        place = arr.at[t, qs, pl.ds(0, (zz + 1) * w)]
        pltpu.make_async_remote_copy(
            src_ref=place, dst_ref=place, send_sem=ll_s.at[g], recv_sem=ll_r.at[g],
            device_id={"kc": me + 2}, device_id_type=MESH).wait_recv()

    def in_segment(g, act):
        t = lax.rem(g, count)
        for size, here, low in (
            (1, (g >= 0) & (g < first), 0),
            (2, ((g >= first) & (g < count)) | ((g >= count + first) & (g < steps)),
             jnp.where(g >= count, 2, 0)),
            (3, (g >= count) & (g < count + first), 1),
        ):
            @pl.when(here)
            def _():
                act(t, pl.ds(low, size))

    def at_place(g, act):
        def body(t, qs):
            mine = total.at[lax.rem(g, ring), pl.ds(0, qs.size)]
            for zz in range(n):
                @pl.when(z == zz)
                def _():
                    act(g, t, qs, mine, zz)

        in_segment(g, body)

    def rightwards(g, t, qs, mine, zz):
        if zz == n - 1:
            return
        value = mine[:, (zz + 1) * w:, :]
        if zz > 0:
            from_left(g, t, qs, zz)
            value += arr[t, qs, (zz + 2) * w:, :].astype(F32)
        out[t, qs, (zz + 1) * w:, :] = value.astype(BF)
        go_right(g, t, qs, zz).start()

    def leftwards(g, t, qs, mine, zz):
        if zz == 0:
            return
        value = mine[:, :zz * w, :]
        if zz < n - 1:
            from_right(g, t, qs, zz)
            value += arr[t, qs, :zz * w, :].astype(F32)
        out[t, qs, :zz * w, :] = value.astype(BF)
        go_left(g, t, qs, zz).start()

    def columns_of(t, whose):
        return pl.ds(pl.multiple_of((2 * t + whose) * rows, rows), rows)

    def keep(g, t, qs):
        return pltpu.make_async_copy(
            kept.at[t, qs], o_ref.at[qs, :, columns_of(t, core)], kept_sem.at[g])

    def give(g, t, qs, whose):
        return pltpu.make_async_remote_copy(
            src_ref=given.at[t, qs], dst_ref=o_ref.at[qs, :, columns_of(t, whose)],
            send_sem=given_s.at[g], recv_sem=given_r.at[g],
            device_id={"kc": partner}, device_id_type=MESH)

    def final(g, t, qs, mine, zz):
        value = mine[:, zz * w:(zz + 1) * w, :]
        if zz == n - 1:
            from_left(g, t, qs, zz)
        if zz > 0:
            value += arr[t, qs, (zz + 1) * w:(zz + 2) * w, :].astype(F32)
        if zz == 0:
            from_right(g, t, qs, zz)
        if zz < n - 1:
            value += arr[t, qs, zz * w:(zz + 1) * w, :].astype(F32)

        @pl.when(core == 0)
        def _():
            kept[t, qs] = value[:, :half]
            given[t, qs] = value[:, half:]

        @pl.when(core == 1)
        def _():
            kept[t, qs] = value[:, half:]
            given[t, qs] = value[:, :half]

    def hand_over(g):
        def body(t, qs):
            keep(g, t, qs).start()
            give(g, t, qs, core).start()

        in_segment(g, body)

    loads = [
        pltpu.make_async_copy(source, target, load_sem.at[i])
        for i, (source, target) in enumerate(((virt_ref, vbuf), (by_b_ref, by_b), (place_ref, place)))
    ]
    for load in loads:
        load.start()
    barrier = pltpu.get_barrier_semaphore()
    signal_all(barrier, "kc", devices)
    signal_all(barrier, "ia", groups)
    mine = pltpu.make_async_copy(
        occ_ref.at[:, pl.ds(pl.multiple_of(me * cols, cols), cols)], occ.at[me], mine_s)
    pl.semaphore_wait(barrier, devices + groups - 2)

    sides(lambda to, kind: direct(to).start())
    for load in loads:
        load.wait()
    lax.fori_loop(0, QUARTERS, prepare, 0)
    send_own(0)
    to_partner().start()
    mine.start()

    def occ_step(e, carry):
        side(e, occ_start)
        side(e - 2, lambda source, kind: occ_spread(source, kind).relay())
        return carry

    lax.fori_loop(0, 2 * n, occ_step, 0)
    for f in range(depth - 1):
        fetch(f).start()
    hops(0, n)
    partner_came()
    sides(lambda source, kind: occ_spread(source, kind).finish())
    mine.wait()

    hop_plan = [(1, 2 * n - 1), (2, 3 * n - 4), (3, 3 * n - 2), (first + 1, 3 * n - 1), (first + 4, 4 * n - 4)]
    relays = [1, 3, first + 3, first + 6]
    makes = [0, 1, 3, first + 4]
    finishes = [1, first + 2, first + 6, count + 2]

    def hops_until(i, after):
        done = most = n
        for at, upto in hop_plan:
            most = max(most, min(upto, QUARTERS * (n - 1)))
            done = jnp.where((i > at) if after else (i >= at), most, done)
        return done

    def at_events(i, events, act):
        here, q = i == events[0], 0
        for later, at in enumerate(events[1:], 1):
            here = here | (i == at)
            q = q + jnp.where(i == at, later, 0)

        @pl.when(here)
        def _():
            act(q)

    def make(q):
        integrals(q)
        each(q, "start")

    def step(i, carry):
        g = i - 2
        at_events(i, relays, lambda q: each(q, "relay"))
        hops(hops_until(i, True), hops_until(i, False))
        at_events(i, makes, make)
        at_events(i, finishes, lambda q: each(q, "finish"))
        in_segment(g, lambda t, qs: multiply(g, t, qs))
        at_place(g - z, rightwards)
        at_place(g - (n - 1 - z), leftwards)
        at_place(g - lag, final)
        hand_over(g - lag)
        return carry

    lax.fori_loop(0, steps + lag + 2, step, 0)

    def drain(g, carry):
        def body(t, qs):
            pair(g, t, qs).wait_send()
            keep(g, t, qs).wait()
            give(g, t, qs, core).wait_send()
            give(g, t, qs, other).wait_recv()
            for zz in range(n):
                @pl.when(z == zz)
                def _():
                    if zz < n - 1:
                        go_right(g, t, qs, zz).wait_send()
                    if zz > 0:
                        go_left(g, t, qs, zz).wait_send()

        in_segment(g, body)
        return carry

    lax.fori_loop(0, steps, drain, 0)
    to_partner().wait_send()
    sides(
        lambda to, kind: direct(to).wait_send(),
        lambda source, kind: occ_spread(source, kind).drain())

    def drain_factors(i, carry):
        q, chip = lax.div(i, n), lax.rem(i, n)
        virtual(q, chip, "pair").wait_send()

        @pl.when((chip <= z) & (z < n - 1))
        def _():
            virtual(q, chip, "right").wait_send()

        @pl.when((chip >= z) & (z > 0))
        def _():
            virtual(q, chip, "left").wait_send()

        @pl.when(chip == 0)
        def _():
            each(q, "drain")

        return carry

    lax.fori_loop(0, QUARTERS * n, drain_factors, 0)


def per_device(amplitudes, occupied, virtual):
    devices, groups = lax.axis_size("kc"), lax.axis_size("ia")
    n = devices // 2
    local_rows, k_width = amplitudes.shape
    q_dim, columns = virtual.shape
    cols = occupied.shape[1] // devices
    k_dim, c_dim, j_own = O // devices, columns // BW, O // devices
    rows = min(512, local_rows // 16)
    count = local_rows // (2 * rows)
    first = count // 4
    depth = 4
    lag = n
    width = n * 2 * (BW // QUARTERS) * j_own
    w = width // n
    dma = pltpu.SemaphoreType.DMA
    hbm = pl.BlockSpec(memory_space=pl.ANY)
    unit = (count, QUARTERS)
    by_b, place = choices(c_dim, j_own)
    result = pl.pallas_call(
        functools.partial(cycle_kernel, devices, groups, count, rows, first, depth, lag),
        out_shape=jax.ShapeDtypeStruct((QUARTERS, w // 2, local_rows), F32),
        in_specs=[hbm] * 5,
        out_specs=hbm,
        scratch_shapes=[
            pltpu.VMEM(by_b.shape, BF),
            pltpu.VMEM(place.shape, BF),
            pltpu.VMEM((c_dim, place.shape[0]), BF),
            pltpu.VMEM((q_dim, columns), BF),
            pltpu.VMEM((columns, devices * q_dim), BF),
            pltpu.VMEM((devices, q_dim, cols), BF),
            pltpu.VMEM((k_dim, groups, c_dim, O * BW), BF),
            pltpu.VMEM((depth, rows, k_width), BF),
            pltpu.VMEM(unit + (rows, LANES), BF),
            pltpu.VMEM(unit + (rows, LANES), BF),
            pltpu.VMEM((lag + 1, 3, width, rows), F32),
            pltpu.VMEM(unit + (width, rows), BF),
            pltpu.VMEM(unit + (width + w, rows), BF),
            pltpu.VMEM(unit + (w // 2, rows), F32),
            pltpu.VMEM(unit + (w // 2, rows), F32),
            dma((3,)), dma(()), dma((devices,)), dma((devices,)),
            dma((devices, groups // 2, 2)), dma((devices, groups // 2, 2)),
            dma((QUARTERS, n)), dma((QUARTERS, n)), dma((QUARTERS, n)), dma((QUARTERS, n)), dma((QUARTERS, n)),
            dma((QUARTERS, 2, groups // 2, 2)), dma((QUARTERS, 2, groups // 2, 2)),
            dma((depth,)),
        ] + [dma((2 * count,))] * 9,
        compiler_params=pltpu.CompilerParams(
            collective_id=0, has_side_effects=True, vmem_limit_bytes=60 * 2**20),
    )(amplitudes, occupied, virtual, by_b, place)
    return result.reshape(BW, j_own, local_rows).transpose(2, 1, 0).reshape(local_rows, j_own * BW)


def solution(mesh):
    placed = (P("ia", "kc"), P("kc", None), P("kc", "ia"))
    return jax.shard_map(
        per_device, mesh=mesh, in_specs=placed, out_specs=P("ia", "kc"), check_vma=False
    )
```

```python
import functools

import jax
import jax.numpy as jnp
import numpy as np
from jax import lax
from jax.experimental import pallas as pl
from jax.experimental.pallas import tpu as pltpu
from jax.sharding import PartitionSpec as P

O = 64
V = 512
BW = 8
QUARTERS = 4
LANES = 128
MESH = pl.DeviceIdType.MESH
BF, F32 = jnp.bfloat16, jnp.float32


class Spread:
    def __init__(self, view, kind, groups, send, recv):
        self.view, self.kind, self.send, self.recv = view, kind, send, recv
        self.a = 2
        self.b = groups // 2
        me = lax.axis_index("ia")
        self.p, self.q = me // self.b, me % self.b

    def at(self, r, s):
        return lax.rem(self.p + s + self.a, self.a) * self.b + lax.rem(self.q + r + self.b, self.b)

    def copy(self, source, r, s, target):
        place = self.view(self.at(*source))
        return pltpu.make_async_remote_copy(
            src_ref=place, dst_ref=place, send_sem=self.send.at[r, s],
            recv_sem=self.recv.at[r, s], device_id={"ia": self.at(*target)}, device_id_type=MESH)

    def sends(self, direct):
        out = []
        for r in range(self.b):
            for s in range(self.a):
                if r and s and not direct:
                    out.append(self.copy((-r, 0), r, s, (0, s)) if self.kind == 0
                               else self.copy((0, -s), r, s, (r, 0)))
                elif (r or s) and not (r and s) and direct:
                    out.append(self.copy((0, 0), r, s, (r, s)))
        return out

    def arrived(self, r, s):
        place = self.view(self.at(-r, -s))
        pltpu.make_async_remote_copy(
            src_ref=place, dst_ref=place, send_sem=self.send.at[r, s], recv_sem=self.recv.at[r, s],
            device_id={"ia": self.at(r, s)}, device_id_type=MESH).wait_recv()

    def start(self):
        order = self.sends(True)
        for copy in order if self.kind else reversed(order):
            copy.start()

    def relay(self):
        if self.kind == 0:
            for r in range(1, self.b):
                self.arrived(r, 0)
        else:
            for s in range(1, self.a):
                self.arrived(0, s)
        for copy in self.sends(False):
            copy.start()

    def finish(self):
        for r in range(self.b):
            for s in range(self.a):
                first = (s == 0) if self.kind == 0 else (r == 0)
                if (r or s) and not first:
                    self.arrived(r, s)

    def drain(self):
        for copy in self.sends(True) + self.sends(False):
            copy.wait_send()


class Direct(Spread):
    def sends(self, direct):
        return [self.copy((0, 0), r, s, (r, s)) for r in range(self.b) for s in range(self.a) if r or s] if direct else []

    def start(self):
        for copy in self.sends(True):
            copy.start()

    def relay(self):
        pass

    def finish(self):
        for r in range(self.b):
            for s in range(self.a):
                if r or s:
                    self.arrived(r, s)


def signal_all(barrier, axis, size):
    me = lax.axis_index(axis)
    for step in range(1, size):
        pl.semaphore_signal(barrier, inc=1, device_id={axis: lax.rem(me + step, size)}, device_id_type=MESH)


def choices(c_dim, j_own):
    per_q, together = BW // QUARTERS, LANES // O
    b, c = np.divmod(np.arange(BW * c_dim), c_dim)
    by_b = np.zeros((BW * c_dim, BW * c_dim), np.float32)
    by_b[np.arange(BW * c_dim), c * BW + b] = 1
    at = np.arange(per_q * LANES)
    b, k, j = at // LANES, at // O % together, at % O
    place = np.zeros((per_q * LANES, together * LANES), np.float32)
    place[at, k * LANES + j // j_own * (per_q * j_own) + b * j_own + j % j_own] = 1
    return jnp.asarray(by_b, BF), jnp.asarray(place, BF)


def cycle_kernel(
    devices, groups, count, rows, first, depth, lag,
    a_ref, occ_ref, virt_ref, by_b_ref, place_ref, o_ref,
    by_b, place, piece, vbuf, vt, occ, cyc, abuf, pair_out, pair_in, total, out, arr, kept, given,
    load_sem, mine_s, o_s, o_r, g_s, g_r, right_s, left_s, v_r, vp_s, vp_r, c_s, c_r,
    a_sem, p_s, p_r, rr_s, rr_r, ll_s, ll_r, kept_sem, given_s, given_r,
):
    n = devices // 2
    me, ia = lax.axis_index("kc"), lax.axis_index("ia")
    z, core = me // 2, me % 2
    other = 1 - core
    partner = z * 2 + other
    q_dim, columns = virt_ref.shape
    per_q = BW // QUARTERS
    c_dim = columns // BW
    q_rows = per_q * c_dim
    share = occ_ref.shape[0] // groups
    cols = occ_ref.shape[1] // devices
    k_dim = cyc.shape[0]
    j_own = O // devices
    w = 2 * per_q * j_own
    half = w // 2
    steps = 2 * count
    ring = total.shape[0]

    def fetch(f):
        slot = lax.rem(f, depth)
        t = lax.rem(f // 2, count)
        chunk = 2 * t + jnp.where(lax.rem(f, 2) == 0, other, core)
        start = pl.multiple_of(chunk * rows, rows)
        return pltpu.make_async_copy(a_ref.at[pl.ds(start, rows)], abuf.at[slot], a_sem.at[slot])

    def lanes_of(device):
        return pl.ds(pl.multiple_of(device * q_dim, q_dim), q_dim)

    def rows_of(q):
        return pl.ds(pl.multiple_of(q * q_rows, q_rows), q_rows)

    def virtual(q, chip, way):
        place = vt.at[rows_of(q), lanes_of(chip * 2 + core)]
        send = {"right": right_s, "left": left_s, "pair": vp_s}[way]
        to = {"right": me + 2, "left": me - 2, "pair": partner}[way]
        recv = vp_r if way == "pair" else v_r
        return pltpu.make_async_remote_copy(
            src_ref=place, dst_ref=place, send_sem=send.at[q, chip],
            recv_sem=recv.at[q, chip], device_id={"kc": to}, device_id_type=MESH)

    def pair_came(q, chip):
        place = vt.at[rows_of(q), lanes_of(chip * 2 + other)]
        pltpu.make_async_remote_copy(
            src_ref=place, dst_ref=place, send_sem=vp_s.at[q, chip], recv_sem=vp_r.at[q, chip],
            device_id={"kc": partner}, device_id_type=MESH).wait_recv()

    def prepare(q, carry):
        vt[rows_of(q), lanes_of(me)] = lax.dot_general(
            by_b[rows_of(q)], vbuf[...], (((1,), (1,)), ((), ())), preferred_element_type=F32).astype(BF)
        return carry

    def send_own(q):
        @pl.when(z < n - 1)
        def _():
            virtual(q, z, "right").start()

        @pl.when(z > 0)
        def _():
            virtual(q, z, "left").start()

        virtual(q, z, "pair").start()

    def hop(q, step):
        @pl.when(z - step >= 0)
        def _():
            virtual(q, z - step, "left").wait_recv()

            @pl.when(z < n - 1)
            def _():
                virtual(q, z - step, "right").start()

            virtual(q, z - step, "pair").start()

        @pl.when(z + step < n)
        def _():
            virtual(q, z + step, "left").wait_recv()

            @pl.when(z > 0)
            def _():
                virtual(q, z + step, "left").start()

            virtual(q, z + step, "pair").start()

    def hops(begin, end):
        def body(h, carry):
            q, dist = h // (n - 1), lax.rem(h, n - 1) + 1
            hop(q, dist)

            @pl.when((dist == jnp.where(q == 0, min(2, n - 1), 1)) & (q < QUARTERS - 1))
            def _():
                send_own(q + 1)

            return carry

        lax.fori_loop(begin, end, body, 0)

    def share_of(i):
        return pl.ds(pl.multiple_of(i * share, share), share)

    def direct(to):
        return pltpu.make_async_remote_copy(
            src_ref=occ_ref.at[pl.ds(pl.multiple_of(ia * share, share), share),
                               pl.ds(pl.multiple_of(to * cols, cols), cols)],
            dst_ref=occ.at[me, share_of(ia)], send_sem=o_s.at[to], recv_sem=o_r.at[me],
            device_id={"kc": to}, device_id_type=MESH)

    def came(source):
        place = occ.at[source, share_of(ia)]
        pltpu.make_async_remote_copy(
            src_ref=place, dst_ref=place, send_sem=o_s.at[source],
            recv_sem=o_r.at[source], device_id={"kc": source}, device_id_type=MESH).wait_recv()

    def to_partner():
        return pltpu.make_async_remote_copy(
            src_ref=occ_ref.at[:, pl.ds(pl.multiple_of(partner * cols, cols), cols)],
            dst_ref=occ.at[me], send_sem=o_s.at[partner], recv_sem=o_r.at[me],
            device_id={"kc": partner}, device_id_type=MESH)

    def partner_came():
        pltpu.make_async_remote_copy(
            src_ref=occ.at[partner], dst_ref=occ.at[partner], send_sem=o_s.at[partner],
            recv_sem=o_r.at[partner], device_id={"kc": partner}, device_id_type=MESH).wait_recv()

    def side(e, act):
        chip = z + (2 * lax.rem(e, 2) - 1) * (lax.div(e, 2) + 1)

        @pl.when((e >= 0) & (chip >= 0) & (chip < n))
        def _():
            act(chip * 2 + core, 0)
            act(chip * 2 + other, 1)

    def sides(*acts):
        def body(e, carry):
            for act in acts:
                side(e, act)
            return carry

        lax.fori_loop(0, 2 * (n - 1), body, 0)

    def occ_spread(source, kind):
        view = functools.partial(lambda source, i: occ.at[source, share_of(i)], source)
        return Direct(view, kind, groups, g_s.at[source], g_r.at[source])

    def occ_start(source, kind):
        came(source)
        occ_spread(source, kind).start()

    def lanes(q, size=1):
        start = q * LANES
        return pl.ds(start if isinstance(q, int) else pl.multiple_of(start, LANES), size * LANES)

    def cycle_spreads(q):
        out = []
        for kind in range(2):
            ks = pl.ds(kind * (k_dim // 2), k_dim // 2)
            view = functools.partial(
                lambda ks, i: cyc.at[ks, i, :, lanes(q)], ks)
            out.append(Spread(view, kind, groups, c_s.at[q, kind], c_r.at[q, kind]))
        return out

    def each(q, what):
        for spread in cycle_spreads(q):
            getattr(spread, what)()

    def integrals(q):
        def waits(chip, carry):
            pair_came(q, chip)
            return carry

        lax.fori_loop(0, n, waits, 0)
        block = jnp.dot(
            vt[rows_of(q), :], occ[...].reshape(-1, cols), preferred_element_type=F32).astype(BF)
        together = LANES // O
        for k in range(0, k_dim, together):
            for b in range(per_q):
                piece[:, b * LANES:(b + 1) * LANES] = block[b * c_dim:(b + 1) * c_dim, k * O:(k + together) * O]
            laid = jnp.dot(piece[...], place[...], preferred_element_type=F32).astype(BF)
            for i in range(together):
                cyc[k + i, ia, :, lanes(q)] = laid[:, i * LANES:(i + 1) * LANES]

    def pair(g, t, qs):
        return pltpu.make_async_remote_copy(
            src_ref=pair_out.at[t, qs], dst_ref=pair_in.at[t, qs], send_sem=p_s.at[g],
            recv_sem=p_r.at[g], device_id={"kc": partner}, device_id_type=MESH)

    def multiply(g, t, qs):
        slot = lax.rem(g, ring)

        def one(i, carry):
            f = 2 * g + i
            fetch(f).wait()

            @pl.when(f + depth - 1 < 2 * steps)
            def _():
                fetch(f + depth - 1).start()

            made = jnp.dot(
                abuf[lax.rem(f, depth)],
                cyc[:, :, :, lanes(qs.start, qs.size)].reshape(-1, qs.size * LANES),
                preferred_element_type=F32)

            @pl.when(i == 0)
            def _():
                for q in range(qs.size):
                    pair_out[t, qs.start + q] = made[:, q * LANES:(q + 1) * LANES].astype(BF)
                pair(g, t, qs).start()

            @pl.when(i == 1)
            def _():
                pair(g, t, qs).wait_recv()
                for q in range(qs.size):
                    both = made[:, q * LANES:(q + 1) * LANES] + pair_in[t, qs.start + q].astype(F32)
                    total[slot, q] = both.T

            return carry

        lax.fori_loop(0, 2, one, 0)

    def go_right(g, t, qs, zz):
        return pltpu.make_async_remote_copy(
            src_ref=out.at[t, qs, pl.ds((zz + 1) * w, (n - 1 - zz) * w)],
            dst_ref=arr.at[t, qs, pl.ds((zz + 2) * w, (n - 1 - zz) * w)],
            send_sem=rr_s.at[g], recv_sem=rr_r.at[g], device_id={"kc": me + 2}, device_id_type=MESH)

    def go_left(g, t, qs, zz):
        return pltpu.make_async_remote_copy(
            src_ref=out.at[t, qs, pl.ds(0, zz * w)], dst_ref=arr.at[t, qs, pl.ds(0, zz * w)],
            send_sem=ll_s.at[g], recv_sem=ll_r.at[g], device_id={"kc": me - 2}, device_id_type=MESH)

    def from_left(g, t, qs, zz):
        place = arr.at[t, qs, pl.ds((zz + 1) * w, (n - zz) * w)]
        pltpu.make_async_remote_copy(
            src_ref=place, dst_ref=place, send_sem=rr_s.at[g], recv_sem=rr_r.at[g],
            device_id={"kc": me - 2}, device_id_type=MESH).wait_recv()

    def from_right(g, t, qs, zz):
        place = arr.at[t, qs, pl.ds(0, (zz + 1) * w)]
        pltpu.make_async_remote_copy(
            src_ref=place, dst_ref=place, send_sem=ll_s.at[g], recv_sem=ll_r.at[g],
            device_id={"kc": me + 2}, device_id_type=MESH).wait_recv()

    def in_segment(g, act):
        t = lax.rem(g, count)
        for size, here, low in (
            (1, (g >= 0) & (g < first), 0),
            (2, ((g >= first) & (g < count)) | ((g >= count + first) & (g < steps)),
             jnp.where(g >= count, 2, 0)),
            (3, (g >= count) & (g < count + first), 1),
        ):
            @pl.when(here)
            def _():
                act(t, pl.ds(low, size))

    def at_place(g, act):
        def body(t, qs):
            mine = total.at[lax.rem(g, ring), pl.ds(0, qs.size)]
            for zz in range(n):
                @pl.when(z == zz)
                def _():
                    act(g, t, qs, mine, zz)

        in_segment(g, body)

    def rightwards(g, t, qs, mine, zz):
        if zz == n - 1:
            return
        value = mine[:, (zz + 1) * w:, :]
        if zz > 0:
            from_left(g, t, qs, zz)
            value += arr[t, qs, (zz + 2) * w:, :].astype(F32)
        out[t, qs, (zz + 1) * w:, :] = value.astype(BF)
        go_right(g, t, qs, zz).start()

    def leftwards(g, t, qs, mine, zz):
        if zz == 0:
            return
        value = mine[:, :zz * w, :]
        if zz < n - 1:
            from_right(g, t, qs, zz)
            value += arr[t, qs, :zz * w, :].astype(F32)
        out[t, qs, :zz * w, :] = value.astype(BF)
        go_left(g, t, qs, zz).start()

    def columns_of(t, whose):
        return pl.ds(pl.multiple_of((2 * t + whose) * rows, rows), rows)

    def keep(g, t, qs):
        return pltpu.make_async_copy(
            kept.at[t, qs], o_ref.at[qs, :, columns_of(t, core)], kept_sem.at[g])

    def give(g, t, qs, whose):
        return pltpu.make_async_remote_copy(
            src_ref=given.at[t, qs], dst_ref=o_ref.at[qs, :, columns_of(t, whose)],
            send_sem=given_s.at[g], recv_sem=given_r.at[g],
            device_id={"kc": partner}, device_id_type=MESH)

    def final(g, t, qs, mine, zz):
        value = mine[:, zz * w:(zz + 1) * w, :]
        if zz == n - 1:
            from_left(g, t, qs, zz)
        if zz > 0:
            value += arr[t, qs, (zz + 1) * w:(zz + 2) * w, :].astype(F32)
        if zz == 0:
            from_right(g, t, qs, zz)
        if zz < n - 1:
            value += arr[t, qs, zz * w:(zz + 1) * w, :].astype(F32)

        @pl.when(core == 0)
        def _():
            kept[t, qs] = value[:, :half]
            given[t, qs] = value[:, half:]

        @pl.when(core == 1)
        def _():
            kept[t, qs] = value[:, half:]
            given[t, qs] = value[:, :half]

    def hand_over(g):
        def body(t, qs):
            keep(g, t, qs).start()
            give(g, t, qs, core).start()

        in_segment(g, body)

    loads = [
        pltpu.make_async_copy(source, target, load_sem.at[i])
        for i, (source, target) in enumerate(((virt_ref, vbuf), (by_b_ref, by_b), (place_ref, place)))
    ]
    for load in loads:
        load.start()
    barrier = pltpu.get_barrier_semaphore()
    signal_all(barrier, "kc", devices)
    signal_all(barrier, "ia", groups)
    mine = pltpu.make_async_copy(
        occ_ref.at[:, pl.ds(pl.multiple_of(me * cols, cols), cols)], occ.at[me], mine_s)
    pl.semaphore_wait(barrier, devices + groups - 2)

    sides(lambda to, kind: direct(to).start())
    for load in loads:
        load.wait()
    lax.fori_loop(0, QUARTERS, prepare, 0)
    send_own(0)
    to_partner().start()
    mine.start()

    def occ_step(e, carry):
        side(e, occ_start)
        side(e - 2, lambda source, kind: occ_spread(source, kind).relay())
        return carry

    lax.fori_loop(0, 2 * n, occ_step, 0)
    for f in range(depth - 1):
        fetch(f).start()
    hops(0, n)
    partner_came()
    sides(lambda source, kind: occ_spread(source, kind).finish())
    mine.wait()

    hop_plan = [(1, 2 * n - 1), (2, 3 * n - 4), (3, 3 * n - 2), (first + 1, 3 * n - 1), (first + 4, 4 * n - 4)]
    relays = [1, 3, first + 3, first + 6]
    makes = [0, 1, 3, first + 4]
    finishes = [1, first + 2, first + 6, count + 2]

    def hops_until(i, after):
        done = most = n
        for at, upto in hop_plan:
            most = max(most, min(upto, QUARTERS * (n - 1)))
            done = jnp.where((i > at) if after else (i >= at), most, done)
        return done

    def at_events(i, events, act):
        here, q = i == events[0], 0
        for later, at in enumerate(events[1:], 1):
            here = here | (i == at)
            q = q + jnp.where(i == at, later, 0)

        @pl.when(here)
        def _():
            act(q)

    def make(q):
        integrals(q)
        each(q, "start")

    def step(i, carry):
        g = i - 2
        at_events(i, relays, lambda q: each(q, "relay"))
        hops(hops_until(i, True), hops_until(i, False))
        at_events(i, makes, make)
        at_events(i, finishes, lambda q: each(q, "finish"))
        in_segment(g, lambda t, qs: multiply(g, t, qs))
        at_place(g - (n - 1 - z), leftwards)
        at_place(g - z, rightwards)
        at_place(g - lag, final)
        hand_over(g - lag)
        return carry

    lax.fori_loop(0, steps + lag + 2, step, 0)

    def drain(g, carry):
        def body(t, qs):
            pair(g, t, qs).wait_send()
            keep(g, t, qs).wait()
            give(g, t, qs, core).wait_send()
            give(g, t, qs, other).wait_recv()
            for zz in range(n):
                @pl.when(z == zz)
                def _():
                    if zz < n - 1:
                        go_right(g, t, qs, zz).wait_send()
                    if zz > 0:
                        go_left(g, t, qs, zz).wait_send()

        in_segment(g, body)
        return carry

    lax.fori_loop(0, steps, drain, 0)
    to_partner().wait_send()
    sides(
        lambda to, kind: direct(to).wait_send(),
        lambda source, kind: occ_spread(source, kind).drain())

    def drain_factors(i, carry):
        q, chip = lax.div(i, n), lax.rem(i, n)
        virtual(q, chip, "pair").wait_send()

        @pl.when((chip <= z) & (z < n - 1))
        def _():
            virtual(q, chip, "right").wait_send()

        @pl.when((chip >= z) & (z > 0))
        def _():
            virtual(q, chip, "left").wait_send()

        @pl.when(chip == 0)
        def _():
            each(q, "drain")

        return carry

    lax.fori_loop(0, QUARTERS * n, drain_factors, 0)


def per_device(amplitudes, occupied, virtual):
    devices, groups = lax.axis_size("kc"), lax.axis_size("ia")
    n = devices // 2
    local_rows, k_width = amplitudes.shape
    q_dim, columns = virtual.shape
    cols = occupied.shape[1] // devices
    k_dim, c_dim, j_own = O // devices, columns // BW, O // devices
    rows = min(512, local_rows // 16)
    count = local_rows // (2 * rows)
    first = count // 4
    depth = 4
    lag = n
    width = n * 2 * (BW // QUARTERS) * j_own
    w = width // n
    dma = pltpu.SemaphoreType.DMA
    hbm = pl.BlockSpec(memory_space=pl.ANY)
    unit = (count, QUARTERS)
    by_b, place = choices(c_dim, j_own)
    result = pl.pallas_call(
        functools.partial(cycle_kernel, devices, groups, count, rows, first, depth, lag),
        out_shape=jax.ShapeDtypeStruct((QUARTERS, w // 2, local_rows), F32),
        in_specs=[hbm] * 5,
        out_specs=hbm,
        scratch_shapes=[
            pltpu.VMEM(by_b.shape, BF),
            pltpu.VMEM(place.shape, BF),
            pltpu.VMEM((c_dim, place.shape[0]), BF),
            pltpu.VMEM((q_dim, columns), BF),
            pltpu.VMEM((columns, devices * q_dim), BF),
            pltpu.VMEM((devices, q_dim, cols), BF),
            pltpu.VMEM((k_dim, groups, c_dim, O * BW), BF),
            pltpu.VMEM((depth, rows, k_width), BF),
            pltpu.VMEM(unit + (rows, LANES), BF),
            pltpu.VMEM(unit + (rows, LANES), BF),
            pltpu.VMEM((lag + 1, 3, width, rows), F32),
            pltpu.VMEM(unit + (width, rows), BF),
            pltpu.VMEM(unit + (width + w, rows), BF),
            pltpu.VMEM(unit + (w // 2, rows), F32),
            pltpu.VMEM(unit + (w // 2, rows), F32),
            dma((3,)), dma(()), dma((devices,)), dma((devices,)),
            dma((devices, groups // 2, 2)), dma((devices, groups // 2, 2)),
            dma((QUARTERS, n)), dma((QUARTERS, n)), dma((QUARTERS, n)), dma((QUARTERS, n)), dma((QUARTERS, n)),
            dma((QUARTERS, 2, groups // 2, 2)), dma((QUARTERS, 2, groups // 2, 2)),
            dma((depth,)),
        ] + [dma((2 * count,))] * 9,
        compiler_params=pltpu.CompilerParams(
            collective_id=0, has_side_effects=True, vmem_limit_bytes=60 * 2**20),
    )(amplitudes, occupied, virtual, by_b, place)
    return result.reshape(BW, j_own, local_rows).transpose(2, 1, 0).reshape(local_rows, j_own * BW)


def solution(mesh):
    placed = (P("ia", "kc"), P("kc", None), P("kc", "ia"))
    return jax.shard_map(
        per_device, mesh=mesh, in_specs=placed, out_specs=P("ia", "kc"), check_vma=False
    )
```
